256 devices in a mesh: chan: 8 (over y, core), row: 32 (over x, z).
Axes of the slice: x: 4, y: 4, z: 8, core: 2. Of those that a mesh axis runs over, the one named last changes fastest.
Arguments:
- voltages: bfloat16 [256, 2, 8, 1024], P('row', None, 'chan'), may hold values from -6 to 6
- kernels: float32 [256, 2, 4], P('row'), may hold values from 0.1 to 1.9
- footprint: int32 [256, 2], P('row'), may hold values from 0 to 252
- cal_weight: float32 [16, 8], P(None, 'chan'), may hold values from -6 to 6
Outputs:
- power_image: float32 [8, 256, 256], P('chan', None, 'row')
- calibrator_maps: float32 [16, 256, 256], P('chan', None, 'row')
The draws below stay inside these ranges and needn't reach their ends.
All inputs are finite; a program needn't handle non-finite values.
Results may differ from the reference program's by a relative error of at most 0.004.
Values may be sent and summed in bfloat16 or wider, within the bound.
No kernel may reach another device: no remote copies, remote signals or barrier semaphores. Data moves between devices by JAX's collectives and lax.ppermute only.
A program may use at most 128 MiB of HBM per device.

```python
import math
import jax
import jax.numpy as jnp
from jax import lax

GRID = 256
KW = 4
S_DEV = 8
NT = 1024
S = 256
CH = 8
Q = 16
ROW_DEV = 8


def draw_footprint(key, part):
    blocks = S // S_DEV
    key_base, key_offsets, key_columns = jax.random.split(jax.random.fold_in(key, 17), 3)
    base = jax.random.randint(key_base, (blocks, 1), 0, blocks - 6)
    base = base.at[0, 0].set(0)
    base = base.at[blocks - 1, 0].set(blocks - 7)
    pairs = jnp.arange(S_DEV, dtype=jnp.int32) // 2
    home = base + 2 * pairs[None, :]
    offsets = jax.random.randint(key_offsets, (blocks, S_DEV), 0, ROW_DEV)
    offsets = offsets.at[:, 1].set(ROW_DEV - 1)
    offsets = offsets.at[0, 0].set(0)
    offsets = offsets.at[blocks - 1, S_DEV - 1].set(ROW_DEV - 1)
    rows_first = jnp.minimum(home * ROW_DEV + offsets, GRID - KW)
    columns_first = jax.random.randint(key_columns, (blocks, S_DEV), 0, GRID - KW + 1)
    columns_first = columns_first.at[0, 0].set(0)
    columns_first = columns_first.at[0, 2].set(GRID - KW)
    return jnp.stack([rows_first.reshape(S), columns_first.reshape(S)], axis=1).astype(jnp.int32)


def shard_levels(stream_key, extent, pieces, smallest, largest):
    level, own = 1.0, jax.random.fold_in(stream_key, 6)
    for position, blocks in pieces:
        steps = jnp.exp(jax.random.uniform(jax.random.fold_in(own, position), (blocks,), jnp.float32, smallest / len(pieces), largest / len(pieces)))
        level = level * jnp.repeat(steps, extent[position] // blocks).reshape([-1 if axis == position else 1 for axis in range(len(extent))])
    return level


def centred(rng, extent, deviation, reach, cuts=(), kind=jnp.bfloat16):
    level = shard_levels(rng, extent, cuts, -0.22, 0.18) if cuts else 1.0
    entries = jax.random.normal(rng, extent, jnp.float32) * deviation * level
    return jnp.minimum(jnp.maximum(entries, -reach), reach).astype(kind)


def setup_inputs(seed: int = 0) -> dict:
    key_list = jax.random.split(jax.random.key(seed), 5)
    return {
        "voltages": centred(key_list[0], (S, 2, CH, NT), 1.0, 6.0, ((0, 32), (2, 8))),
        "kernels": jnp.clip(1.0 + 0.18 * jax.random.normal(key_list[1], (S, 2, KW), jnp.float32), 0.1, 1.9),
        "footprint": draw_footprint(jax.random.fold_in(key_list[4], 71), 0),
        "cal_weight": centred(key_list[3], (Q, CH), 1.0, 6.0, ((1, 8),), jnp.float32),
    }


def dft_tables(size, first, count):
    indices = jnp.arange(size, dtype=jnp.int32)
    columns = first + jnp.arange(count, dtype=jnp.int32)
    phases = (indices[:, None] * columns[None, :]) % size
    angles = phases.astype(jnp.float32) * (2.0 * math.pi / size)
    return jnp.cos(angles), jnp.sin(angles)


def placed(weights, starts, first, count):
    positions = first + jnp.arange(count, dtype=jnp.int32)
    taps = jnp.arange(weights.shape[1], dtype=jnp.int32)
    target = starts[:, None] + taps[None, :]
    hit = positions[None, None, :] == target[:, :, None]
    return jnp.sum(jnp.where(hit, weights[:, :, None], jnp.zeros((), weights.dtype)), axis=1)


def blocked_time_sum(values):
    samples = values.shape[-1]
    width = math.gcd(samples, 128)
    shaped = values.reshape(values.shape[:-1] + (samples // width, width))
    return jnp.sum(jnp.sum(shaped, axis=-1), axis=-1)


def reference(voltages, kernels, footprint, cal_weight):
    highest = lax.Precision.HIGHEST
    row_weight = placed(kernels[:, 0, :], footprint[:, 0], 0, GRID)
    col_weight = placed(kernels[:, 1, :], footprint[:, 1], 0, GRID)
    cos_table, sin_table = dft_tables(GRID, 0, GRID)
    power_scale = 1.0 / (2.0 * NT * S * KW * KW)
    by_channel = jnp.moveaxis(voltages.astype(jnp.float32), 2, 0)

    def one_channel(volt_block):
        volt_real = volt_block[:, 0, :]
        volt_imag = volt_block[:, 1, :]
        spread_real = row_weight.T[:, :, None] * volt_real[None, :, :]
        spread_imag = row_weight.T[:, :, None] * volt_imag[None, :, :]
        grid_real = jnp.einsum('ust,sv->uvt', spread_real, col_weight, precision=highest)
        grid_imag = jnp.einsum('ust,sv->uvt', spread_imag, col_weight, precision=highest)
        half_real = (jnp.einsum('uvt,vm->umt', grid_real, cos_table, precision=highest)
                     + jnp.einsum('uvt,vm->umt', grid_imag, sin_table, precision=highest))
        half_imag = (jnp.einsum('uvt,vm->umt', grid_imag, cos_table, precision=highest)
                     - jnp.einsum('uvt,vm->umt', grid_real, sin_table, precision=highest))
        sky_real = (jnp.einsum('umt,ul->lmt', half_real, cos_table, precision=highest)
                    + jnp.einsum('umt,ul->lmt', half_imag, sin_table, precision=highest))
        sky_imag = (jnp.einsum('umt,ul->lmt', half_imag, cos_table, precision=highest)
                    - jnp.einsum('umt,ul->lmt', half_real, sin_table, precision=highest))
        return blocked_time_sum(sky_real * sky_real + sky_imag * sky_imag) * power_scale

    power_image = lax.map(one_channel, by_channel)
    calibrator_maps = jnp.einsum('qc,clm->qlm', cal_weight, power_image, precision=highest)
    return power_image, calibrator_maps
```

```python
import functools
import math

import jax
import jax.numpy as jnp
import numpy as np
from jax import lax
from jax.experimental import pallas as pl
from jax.experimental.pallas import tpu as pltpu
from jax.sharding import PartitionSpec as P

GRID = 256
LANES = 128
BF16 = jnp.bfloat16
F32 = jnp.float32


def transform_tables():
    index = np.arange(GRID)
    angles = (index[:, None] * index[None, :] % GRID) * (2.0 * math.pi / GRID)
    exact = np.concatenate([np.cos(angles), np.sin(angles)], axis=1).astype(np.float32)
    high = exact.astype(BF16)
    low = (exact - high.astype(np.float32)).astype(BF16)
    return np.concatenate([high, low], axis=1)


def rounded(values):
    return values.astype(BF16).astype(F32)


def pack_kernel(peers, volt_ref, kern_ref, foot_ref, out_ref, turn_ref):
    stations, _, samples = volt_ref.shape
    taps = kern_ref.shape[1]
    turn_ref[...] = jnp.zeros_like(turn_ref)
    for axis in range(2):
        weights = kern_ref[axis]
        high = rounded(weights)
        turn_ref[axis * taps : (axis + 1) * taps, :stations] = high
        turn_ref[(2 + axis) * taps : (3 + axis) * taps, :stations] = weights - high
    turn_ref[4 * taps : 4 * taps + 2, :stations] = foot_ref[...].astype(F32)
    extra = turn_ref[...].T[:stations].astype(BF16)
    real = volt_ref[:, 0, :]
    imag = volt_ref[:, 1, :]
    for peer in range(peers):
        out_ref[peer, :, :samples] = real
        out_ref[peer, :, samples : 2 * samples] = imag
        out_ref[peer, :, 2 * samples :] = extra


def spread(taps_ref, start, first, count):
    taps = [taps_ref[:, start + k : start + k + 1] for k in range(count)]
    offset = lax.broadcasted_iota(jnp.int32, (first.shape[0], GRID), 1).astype(F32) - first
    out = jnp.zeros_like(offset)
    for k in range(count):
        out = jnp.where(offset == float(k), taps[k], out)
    return out.astype(BF16)


def image_kernel(taps, share, scale, row_of, gathered_ref, tables_ref, weight_ref, power_ref, send_ref,
                 extra_ref, beam_ref, exact_ref):
    stations = gathered_ref.shape[0]
    samples = (gathered_ref.shape[1] - LANES) // 2
    peers = send_ref.shape[0]
    per_peer = weight_ref.shape[0] // peers
    row = row_of()

    both = gathered_ref[:, : 2 * samples]
    real = gathered_ref[:, :samples]
    imag = gathered_ref[:, samples : 2 * samples]
    outer = (((1,), (1,)), ((), ()))
    corr_real = lax.dot_general(both, both, outer, preferred_element_type=F32)
    half = lax.dot_general(imag, real, outer, preferred_element_type=F32)
    corr_imag = half - half.T
    corr_real = corr_real.astype(BF16)
    corr_both = jnp.concatenate([corr_real, (2.0 * corr_imag).astype(BF16)], axis=1)

    extra_ref[...] = gathered_ref[:, 2 * samples :].astype(F32)
    first_row = extra_ref[:, 4 * taps : 4 * taps + 1]
    first_col = extra_ref[:, 4 * taps + 1 : 4 * taps + 2]
    high = jnp.concatenate(
        [spread(extra_ref, 0, first_row, taps), spread(extra_ref, taps, first_col, taps)], axis=0
    )
    low = jnp.concatenate(
        [spread(extra_ref, 2 * taps, first_row, taps), spread(extra_ref, 3 * taps, first_col, taps)],
        axis=0,
    )
    table_high = tables_ref[:, : 2 * GRID]
    table_low = tables_ref[:, 2 * GRID :]
    response = (
        jnp.dot(high, table_high, preferred_element_type=F32)
        + jnp.dot(high, table_low, preferred_element_type=F32)
        + jnp.dot(low, table_high, preferred_element_type=F32)
    )
    row_real = response[:stations, :GRID]
    row_imag = response[:stations, GRID:]
    first = row * share
    upper = first >= LANES
    turn = lax.rem(2 * LANES - first, LANES)
    column = response[stations:]
    col_real = pltpu.roll(
        jnp.where(upper, column[:, LANES : 2 * LANES], column[:, :LANES]), turn, 1
    )
    col_imag = pltpu.roll(
        jnp.where(upper, column[:, 3 * LANES :], column[:, 2 * LANES : 3 * LANES]), turn, 1
    )

    for m in range(share):
        c_real = col_real[:, m : m + 1]
        c_imag = col_imag[:, m : m + 1]
        beam_real = c_real * row_real - c_imag * row_imag
        beam_imag = c_real * row_imag + c_imag * row_real
        exact_ref[m, 0] = beam_real
        exact_ref[m, 1] = beam_imag
        beam_ref[m, :stations] = beam_imag.astype(BF16)
        beam_ref[m, stations:] = beam_real.astype(BF16)
        sum_real = jnp.dot(corr_real, beam_ref[m, stations:], preferred_element_type=F32)
        sum_imag = jnp.dot(corr_both, beam_ref[m], preferred_element_type=F32)
        total = exact_ref[m, 0] * sum_real + exact_ref[m, 1] * sum_imag
        power = jnp.sum(total, axis=0, keepdims=True) * scale
        power_ref[m : m + 1, :] = power
    power = power_ref[...]
    for peer in range(peers):
        for q in range(per_peer):
            send_ref[peer, q * share : (q + 1) * share, :] = power * weight_ref[peer * per_peer + q, 0]


def vmem():
    return pl.BlockSpec(memory_space=pltpu.VMEM)


def packed(volt, kern, foot, peers):
    stations, _, samples = volt.shape
    return pl.pallas_call(
        functools.partial(pack_kernel, peers),
        out_shape=jax.ShapeDtypeStruct((peers, stations, 2 * samples + LANES), BF16),
        in_specs=[vmem()] * 3,
        out_specs=vmem(),
        scratch_shapes=[pltpu.VMEM((LANES, LANES), F32)],
        compiler_params=pltpu.CompilerParams(vmem_limit_bytes=8 << 20),
        name="pack",
    )(volt, kern, foot)


def imaged(gathered, tables, weight, peers, taps, share, scale, row_of, interpret=False):
    stations = gathered.shape[0]
    return pl.pallas_call(
        functools.partial(image_kernel, taps, share, scale, row_of),
        out_shape=(
            jax.ShapeDtypeStruct((share, GRID), F32),
            jax.ShapeDtypeStruct((peers, weight.shape[0] // peers * share, GRID), F32),
        ),
        in_specs=[vmem(), vmem(), pl.BlockSpec(memory_space=pltpu.SMEM)],
        out_specs=(vmem(), vmem()),
        scratch_shapes=[
            pltpu.VMEM((stations, LANES), F32),
            pltpu.VMEM((share, 2 * stations, GRID), BF16),
            pltpu.VMEM((share, 2, stations, GRID), F32),
        ],
        compiler_params=pltpu.CompilerParams(vmem_limit_bytes=24 << 20),
        name="image",
        interpret=interpret,
    )(gathered, tables, weight)


def on_device(tables, voltages, kernels, footprint, cal_weight):
    local_stations, _, local_channels, samples = voltages.shape
    rows = lax.axis_size("row")
    channels = lax.axis_size("chan")
    share = GRID // rows
    taps = kernels.shape[2]
    station_count = local_stations * rows
    scale = 1.0 / (2.0 * samples * station_count * taps * taps)
    volt = voltages.reshape(local_stations, 2, samples)
    send = packed(volt, jnp.transpose(kernels, (1, 2, 0)), footprint.T, rows)
    gathered = lax.all_to_all(send, "row", 0, 0, tiled=True)
    gathered = gathered.reshape(station_count, 2 * samples + LANES)
    power, weighted = imaged(
        gathered, tables, cal_weight, channels, taps, share, scale, lambda: lax.axis_index("row")
    )
    parts = lax.all_to_all(weighted, "chan", 0, 0, tiled=True)
    maps = jnp.sum(parts, axis=0).reshape(-1, share, GRID)
    return jnp.transpose(power[None], (0, 2, 1)), jnp.transpose(maps, (0, 2, 1))


def solution(mesh):
    specs = (P("row", None, "chan", None), P("row", None, None), P("row", None), P(None, "chan"))
    tables = transform_tables()
    return jax.shard_map(
        lambda *args: on_device(jnp.asarray(tables), *args),
        mesh=mesh,
        in_specs=specs,
        out_specs=(P("chan", None, "row"), P("chan", None, "row")),
        check_vma=False,
    )
```

```python
import functools
import math

import jax
import jax.numpy as jnp
import numpy as np
from jax import lax
from jax.experimental import pallas as pl
from jax.experimental.pallas import tpu as pltpu
from jax.sharding import PartitionSpec as P

GRID = 256
LANES = 128
BF16 = jnp.bfloat16
F32 = jnp.float32


def transform_tables():
    index = np.arange(GRID)
    angles = (index[:, None] * index[None, :] % GRID) * (2.0 * math.pi / GRID)
    exact = np.concatenate([np.cos(angles), np.sin(angles)], axis=1).astype(np.float32)
    high = exact.astype(BF16)
    low = (exact - high.astype(np.float32)).astype(BF16)
    return np.concatenate([high, low], axis=1)


def rounded(values):
    return values.astype(BF16).astype(F32)


def pack_kernel(peers, volt_hbm, kern_hbm, foot_hbm, out_ref, turn_ref, volt_ref, kern_ref, foot_ref, sems):
    sources = ((kern_hbm, kern_ref), (foot_hbm, foot_ref), (volt_hbm, volt_ref))
    copies = [pltpu.make_async_copy(*pair, sems.at[i]) for i, pair in enumerate(sources)]
    for copy in copies:
        copy.start()
    for copy in copies:
        copy.wait()
    stations, _, samples = volt_ref.shape
    taps = kern_ref.shape[1]
    turn_ref[...] = jnp.zeros_like(turn_ref)
    for axis in range(2):
        weights = kern_ref[axis]
        high = rounded(weights)
        turn_ref[axis * taps : (axis + 1) * taps, :stations] = high
        turn_ref[(2 + axis) * taps : (3 + axis) * taps, :stations] = weights - high
    turn_ref[4 * taps : 4 * taps + 2, :stations] = foot_ref[...].astype(F32)
    extra = turn_ref[...].T[:stations].astype(BF16)
    real = volt_ref[:, 0, :]
    imag = volt_ref[:, 1, :]
    for peer in range(peers):
        out_ref[peer, :, :samples] = real
        out_ref[peer, :, samples : 2 * samples] = imag
        out_ref[peer, :, 2 * samples :] = extra


def spread(taps_ref, start, first, count):
    taps = [taps_ref[:, start + k : start + k + 1] for k in range(count)]
    offset = lax.broadcasted_iota(jnp.int32, (first.shape[0], GRID), 1).astype(F32) - first
    out = jnp.zeros_like(offset)
    for k in range(count):
        out = jnp.where(offset == float(k), taps[k], out)
    return out.astype(BF16)


def image_kernel(taps, share, scale, row_of, gathered_ref, tables_ref, weight_ref, power_ref, send_ref,
                 extra_ref, beam_ref, exact_ref):
    stations = gathered_ref.shape[0]
    samples = (gathered_ref.shape[1] - LANES) // 2
    peers = send_ref.shape[0]
    per_peer = weight_ref.shape[1] // peers
    row = row_of()

    both = gathered_ref[:, : 2 * samples]
    real = gathered_ref[:, :samples]
    imag = gathered_ref[:, samples : 2 * samples]
    outer = (((1,), (1,)), ((), ()))
    corr_real = lax.dot_general(both, both, outer, preferred_element_type=F32)
    half = lax.dot_general(imag, real, outer, preferred_element_type=F32)
    corr_imag = half - half.T
    corr_real = corr_real.astype(BF16)
    corr_both = jnp.concatenate([corr_real, (2.0 * corr_imag).astype(BF16)], axis=1)

    extra_ref[...] = gathered_ref[:, 2 * samples :].astype(F32)
    first_row = extra_ref[:, 4 * taps : 4 * taps + 1]
    first_col = extra_ref[:, 4 * taps + 1 : 4 * taps + 2]
    high = jnp.concatenate(
        [spread(extra_ref, 0, first_row, taps), spread(extra_ref, taps, first_col, taps)], axis=0
    )
    low = jnp.concatenate(
        [spread(extra_ref, 2 * taps, first_row, taps), spread(extra_ref, 3 * taps, first_col, taps)],
        axis=0,
    )
    table_high = tables_ref[:, : 2 * GRID]
    table_low = tables_ref[:, 2 * GRID :]
    response = (
        jnp.dot(high, table_high, preferred_element_type=F32)
        + jnp.dot(high, table_low, preferred_element_type=F32)
        + jnp.dot(low, table_high, preferred_element_type=F32)
    )
    row_real = response[:stations, :GRID]
    row_imag = response[:stations, GRID:]
    first = row * share
    upper = first >= LANES
    turn = lax.rem(2 * LANES - first, LANES)
    column = response[stations:]
    col_real = pltpu.roll(
        jnp.where(upper, column[:, LANES : 2 * LANES], column[:, :LANES]), turn, 1
    )
    col_imag = pltpu.roll(
        jnp.where(upper, column[:, 3 * LANES :], column[:, 2 * LANES : 3 * LANES]), turn, 1
    )

    for m in range(share):
        c_real = col_real[:, m : m + 1]
        c_imag = col_imag[:, m : m + 1]
        beam_real = c_real * row_real - c_imag * row_imag
        beam_imag = c_real * row_imag + c_imag * row_real
        exact_ref[m, 0] = beam_real
        exact_ref[m, 1] = beam_imag
        beam_ref[m, :stations] = beam_imag.astype(BF16)
        beam_ref[m, stations:] = beam_real.astype(BF16)
        sum_real = jnp.dot(corr_real, beam_ref[m, stations:], preferred_element_type=F32)
        sum_imag = jnp.dot(corr_both, beam_ref[m], preferred_element_type=F32)
        total = exact_ref[m, 0] * sum_real + exact_ref[m, 1] * sum_imag
        power = jnp.sum(total, axis=0, keepdims=True) * scale
        power_ref[m : m + 1, :] = power
    power = power_ref[...]
    for peer in range(peers):
        for q in range(per_peer):
            send_ref[peer, q * share : (q + 1) * share, :] = power * weight_ref[0, peer * per_peer + q]


def vmem():
    return pl.BlockSpec(memory_space=pltpu.VMEM)


def packed(volt, kern, foot, peers):
    stations, _, samples = volt.shape
    return pl.pallas_call(
        functools.partial(pack_kernel, peers),
        out_shape=jax.ShapeDtypeStruct((peers, stations, 2 * samples + LANES), BF16),
        in_specs=[pl.BlockSpec(memory_space=pltpu.HBM)] * 3,
        out_specs=vmem(),
        scratch_shapes=[pltpu.VMEM((LANES, LANES), F32)]
        + [pltpu.VMEM(x.shape, x.dtype) for x in (volt, kern, foot)]
        + [pltpu.SemaphoreType.DMA((3,))],
        compiler_params=pltpu.CompilerParams(vmem_limit_bytes=8 << 20),
        name="pack",
    )(volt, kern, foot)


def imaged(gathered, tables, weight, peers, taps, share, scale, row_of, interpret=False):
    stations = gathered.shape[0]
    return pl.pallas_call(
        functools.partial(image_kernel, taps, share, scale, row_of),
        out_shape=(
            jax.ShapeDtypeStruct((share, GRID), F32),
            jax.ShapeDtypeStruct((peers, weight.shape[1] // peers * share, GRID), F32),
        ),
        in_specs=[vmem(), vmem(), pl.BlockSpec(memory_space=pltpu.SMEM)],
        out_specs=(vmem(), vmem()),
        scratch_shapes=[
            pltpu.VMEM((stations, LANES), F32),
            pltpu.VMEM((share, 2 * stations, GRID), BF16),
            pltpu.VMEM((share, 2, stations, GRID), F32),
        ],
        compiler_params=pltpu.CompilerParams(vmem_limit_bytes=24 << 20),
        name="image",
        interpret=interpret,
    )(gathered, tables, weight)


def on_device(tables, voltages, kernels, footprint, cal_weight):
    local_stations, _, local_channels, samples = voltages.shape
    rows = lax.axis_size("row")
    channels = lax.axis_size("chan")
    share = GRID // rows
    taps = kernels.shape[2]
    station_count = local_stations * rows
    scale = 1.0 / (2.0 * samples * station_count * taps * taps)
    volt = voltages.reshape(local_stations, 2, samples)
    send = packed(volt, jnp.transpose(kernels, (1, 2, 0)), footprint.T, rows)
    gathered = lax.all_to_all(send, "row", 0, 0, tiled=True)
    gathered = gathered.reshape(station_count, 2 * samples + LANES)
    power, weighted = imaged(
        gathered, tables, cal_weight.T, channels, taps, share, scale, lambda: lax.axis_index("row")
    )
    parts = lax.all_to_all(weighted, "chan", 0, 0, tiled=True)
    maps = jnp.sum(parts, axis=0).reshape(-1, share, GRID)
    return jnp.transpose(power[None], (0, 2, 1)), jnp.transpose(maps, (0, 2, 1))


def solution(mesh):
    specs = (P("row", None, "chan", None), P("row", None, None), P("row", None), P(None, "chan"))
    tables = transform_tables()
    return jax.shard_map(
        lambda *args: on_device(jnp.asarray(tables), *args),
        mesh=mesh,
        in_specs=specs,
        out_specs=(P("chan", None, "row"), P("chan", None, "row")),
        check_vma=False,
    )
```

```python
import functools
import math

import jax
import jax.numpy as jnp
import numpy as np
from jax import lax
from jax.experimental import pallas as pl
from jax.experimental.pallas import tpu as pltpu
from jax.sharding import PartitionSpec as P

GRID = 256
LANES = 128
SPLIT = 2
BF16 = jnp.bfloat16
F32 = jnp.float32


def transform_tables():
    index = np.arange(GRID)
    angles = (index[:, None] * index[None, :] % GRID) * (2.0 * math.pi / GRID)
    exact = np.concatenate([np.cos(angles), np.sin(angles)], axis=1).astype(np.float32)
    high = exact.astype(BF16)
    low = (exact - high.astype(np.float32)).astype(BF16)
    return np.concatenate([high, low], axis=1)


def rounded(values):
    return values.astype(BF16).astype(F32)


def pack_kernel(peers, split, volt_ref, small_ref, out_ref, turn_ref):
    stations, _, samples = volt_ref.shape
    part = samples // split
    weights = small_ref.shape[0] - 2
    turn_ref[...] = jnp.zeros_like(turn_ref)
    values = small_ref[...]
    high = rounded(values[:weights])
    turn_ref[:weights, :stations] = high
    turn_ref[weights : 2 * weights, :stations] = values[:weights] - high
    turn_ref[2 * weights : 2 * weights + 2, :stations] = values[weights:]
    extra = turn_ref[...].T[:stations].astype(BF16)
    real = volt_ref[:, 0, :]
    imag = volt_ref[:, 1, :]
    for peer in range(peers):
        start = (peer % split) * part
        out_ref[peer, :, :part] = real[:, start : start + part]
        out_ref[peer, :, part : 2 * part] = imag[:, start : start + part]
        out_ref[peer, :, 2 * part :] = extra


def spread(taps_ref, start, first, count):
    taps = [taps_ref[:, start + k : start + k + 1] for k in range(count)]
    offset = lax.broadcasted_iota(jnp.int32, (first.shape[0], GRID), 1).astype(F32) - first
    out = jnp.zeros_like(offset)
    for k in range(count):
        out = jnp.where(offset == float(k), taps[k], out)
    return out.astype(BF16)


def image_kernel(taps, share, split, scale, place_of, gathered_ref, tables_ref, weight_ref, send_ref,
                 extra_ref, beam_ref, exact_ref, power_ref):
    stations = gathered_ref.shape[0]
    samples = (gathered_ref.shape[1] - LANES) // 2
    peers = send_ref.shape[0] // split
    per_peer = weight_ref.shape[1] // peers
    channel, row = place_of()

    both = gathered_ref[:, : 2 * samples]
    real = gathered_ref[:, :samples]
    imag = gathered_ref[:, samples : 2 * samples]
    outer = (((1,), (1,)), ((), ()))
    corr_real = lax.dot_general(both, both, outer, preferred_element_type=F32)
    half = lax.dot_general(imag, real, outer, preferred_element_type=F32)
    corr_imag = half - half.T
    corr_real = corr_real.astype(BF16)
    corr_both = jnp.concatenate([corr_real, (2.0 * corr_imag).astype(BF16)], axis=1)

    extra_ref[...] = gathered_ref[:, 2 * samples :].astype(F32)
    first_row = extra_ref[:, 4 * taps : 4 * taps + 1]
    first_col = extra_ref[:, 4 * taps + 1 : 4 * taps + 2]
    high = jnp.concatenate(
        [spread(extra_ref, 0, first_row, taps), spread(extra_ref, taps, first_col, taps)], axis=0
    )
    low = jnp.concatenate(
        [spread(extra_ref, 2 * taps, first_row, taps), spread(extra_ref, 3 * taps, first_col, taps)],
        axis=0,
    )
    table_high = tables_ref[:, : 2 * GRID]
    table_low = tables_ref[:, 2 * GRID :]
    response = (
        jnp.dot(high, table_high, preferred_element_type=F32)
        + jnp.dot(high, table_low, preferred_element_type=F32)
        + jnp.dot(low, table_high, preferred_element_type=F32)
    )
    row_real = response[:stations, :GRID]
    row_imag = response[:stations, GRID:]
    first = row // split * (split * share)
    upper = first >= LANES
    turn = lax.rem(2 * LANES - first, LANES)
    column = response[stations:]
    col_real = pltpu.roll(
        jnp.where(upper, column[:, LANES : 2 * LANES], column[:, :LANES]), turn, 1
    )
    col_imag = pltpu.roll(
        jnp.where(upper, column[:, 3 * LANES :], column[:, 2 * LANES : 3 * LANES]), turn, 1
    )

    for m in range(share * split):
        c_real = col_real[:, m : m + 1]
        c_imag = col_imag[:, m : m + 1]
        beam_real = c_real * row_real - c_imag * row_imag
        beam_imag = c_real * row_imag + c_imag * row_real
        exact_ref[m, 0] = beam_real
        exact_ref[m, 1] = beam_imag
        beam_ref[m, :stations] = beam_imag.astype(BF16)
        beam_ref[m, stations:] = beam_real.astype(BF16)
        sum_real = jnp.dot(corr_real, beam_ref[m, stations:], preferred_element_type=F32)
        sum_imag = jnp.dot(corr_both, beam_ref[m], preferred_element_type=F32)
        total = exact_ref[m, 0] * sum_real + exact_ref[m, 1] * sum_imag
        power_ref[m : m + 1, :] = jnp.sum(total, axis=0, keepdims=True) * scale
    for side in range(split):
        power = power_ref[side * share : (side + 1) * share, :]
        for peer in range(peers):
            for q in range(per_peer):
                factor = jnp.where(channel == peer, 1.0, weight_ref[0, peer * per_peer + q])
                send_ref[peer * split + side, q * share : (q + 1) * share, :] = power * factor


def finish_kernel(split, channel_of, parts_ref, weight_ref, power_ref, maps_ref):
    share = power_ref.shape[0]
    per_peer = maps_ref.shape[0] // share
    channel = channel_of()
    peers = parts_ref.shape[0] // split
    power = jnp.zeros(power_ref.shape, F32)
    for side in range(split):
        power += parts_ref[channel * split + side, :share]
    power_ref[...] = power
    for q in range(per_peer):
        total = power * weight_ref[0, channel * per_peer + q]
        for peer in range(peers):
            for side in range(split):
                block = parts_ref[peer * split + side, q * share : (q + 1) * share]
                total += jnp.where(channel == peer, 0.0, block)
        maps_ref[q * share : (q + 1) * share] = total


def vmem():
    return pl.BlockSpec(memory_space=pltpu.VMEM)


def smem():
    return pl.BlockSpec(memory_space=pltpu.SMEM)


def packed(volt, small, peers, split):
    stations, _, samples = volt.shape
    return pl.pallas_call(
        functools.partial(pack_kernel, peers, split),
        out_shape=jax.ShapeDtypeStruct((peers, stations, 2 * samples // split + LANES), BF16),
        in_specs=[vmem()] * 2,
        out_specs=vmem(),
        scratch_shapes=[pltpu.VMEM((LANES, LANES), F32)],
        compiler_params=pltpu.CompilerParams(vmem_limit_bytes=8 << 20),
        name="pack",
    )(volt, small)


def imaged(gathered, tables, weight, peers, taps, share, split, scale, place_of, interpret=False):
    stations = gathered.shape[0]
    columns = share * split
    return pl.pallas_call(
        functools.partial(image_kernel, taps, share, split, scale, place_of),
        out_shape=jax.ShapeDtypeStruct((peers * split, weight.shape[1] // peers * share, GRID), F32),
        in_specs=[vmem(), vmem(), smem()],
        out_specs=vmem(),
        scratch_shapes=[
            pltpu.VMEM((stations, LANES), F32),
            pltpu.VMEM((columns, 2 * stations, GRID), BF16),
            pltpu.VMEM((columns, 2, stations, GRID), F32),
            pltpu.VMEM((columns, GRID), F32),
        ],
        compiler_params=pltpu.CompilerParams(vmem_limit_bytes=32 << 20),
        name="image",
        interpret=interpret,
    )(gathered, tables, weight)


def finished(parts, weight, share, split, channel_of, interpret=False):
    return pl.pallas_call(
        functools.partial(finish_kernel, split, channel_of),
        out_shape=(
            jax.ShapeDtypeStruct((share, GRID), F32),
            jax.ShapeDtypeStruct((parts.shape[1], GRID), F32),
        ),
        in_specs=[vmem(), smem()],
        out_specs=(vmem(), vmem()),
        compiler_params=pltpu.CompilerParams(vmem_limit_bytes=8 << 20),
        name="finish",
        interpret=interpret,
    )(parts, weight)


def on_device(tables, voltages, kernels, footprint, cal_weight):
    local_stations, _, local_channels, samples = voltages.shape
    rows = lax.axis_size("row")
    channels = lax.axis_size("chan")
    share = GRID // rows
    taps = kernels.shape[2]
    station_count = local_stations * rows
    scale = 1.0 / (2.0 * samples * station_count * taps * taps)
    volt = voltages.reshape(local_stations, 2, samples)
    small = jnp.concatenate(
        [jnp.transpose(kernels, (1, 2, 0)).reshape(2 * taps, -1), footprint.T.astype(F32)], axis=0
    )
    send = packed(volt, small, rows, SPLIT)
    gathered = lax.all_to_all(send, "row", 0, 0, tiled=True)
    gathered = gathered.reshape(station_count, -1)
    weight = cal_weight.T
    weighted = imaged(
        gathered, tables, weight, channels, taps, share, SPLIT, scale,
        lambda: (lax.axis_index("chan"), lax.axis_index("row")),
    )
    groups = [
        [c * rows + first + side for c in range(channels) for side in range(SPLIT)]
        for first in range(0, rows, SPLIT)
    ]
    parts = lax.all_to_all(
        weighted, ("chan", "row"), 0, 0, axis_index_groups=groups, tiled=True
    )
    power, maps = finished(parts, weight, share, SPLIT, lambda: lax.axis_index("chan"))
    maps = maps.reshape(-1, share, GRID)
    return jnp.transpose(power[None], (0, 2, 1)), jnp.transpose(maps, (0, 2, 1))


def solution(mesh):
    specs = (P("row", None, "chan", None), P("row", None, None), P("row", None), P(None, "chan"))
    tables = transform_tables()
    return jax.shard_map(
        lambda *args: on_device(jnp.asarray(tables), *args),
        mesh=mesh,
        in_specs=specs,
        out_specs=(P("chan", None, "row"), P("chan", None, "row")),
        check_vma=False,
    )
```

```python
import functools
import math

import jax
import jax.numpy as jnp
import numpy as np
from jax import lax
from jax.experimental import pallas as pl
from jax.experimental.pallas import tpu as pltpu
from jax.sharding import PartitionSpec as P

GRID = 256
LANES = 128
SPLIT = 2
BF16 = jnp.bfloat16
F32 = jnp.float32


def transform_tables():
    index = np.arange(GRID)
    angles = (index[:, None] * index[None, :] % GRID) * (2.0 * math.pi / GRID)
    exact = np.concatenate([np.cos(angles), np.sin(angles)], axis=1).astype(np.float32)
    high = exact.astype(BF16)
    low = (exact - high.astype(np.float32)).astype(BF16)
    return np.concatenate([high, low], axis=1)


def rounded(values):
    return values.astype(BF16).astype(F32)


def pack_kernel(peers, split, volt_hbm, kern_hbm, foot_hbm, gain_hbm, out_ref, weight_ref,
                turn_ref, volt_ref, kern_ref, foot_ref, sems):
    pairs = ((kern_hbm, kern_ref), (foot_hbm, foot_ref), (gain_hbm, weight_ref), (volt_hbm, volt_ref))
    copies = [pltpu.make_async_copy(*pair, sems.at[i]) for i, pair in enumerate(pairs)]
    for copy in copies:
        copy.start()
    stations, _, samples = volt_ref.shape
    part = samples // split
    taps = kern_ref.shape[1]
    turn_ref[...] = jnp.zeros_like(turn_ref)
    for copy in copies:
        copy.wait()
    for axis in range(2):
        values = kern_ref[axis]
        high = rounded(values)
        turn_ref[axis * taps : (axis + 1) * taps, :stations] = high
        turn_ref[(2 + axis) * taps : (3 + axis) * taps, :stations] = values - high
    turn_ref[4 * taps : 4 * taps + 2, :stations] = foot_ref[...].astype(F32)
    extra = turn_ref[...].T[:stations].astype(BF16)
    real = volt_ref[:, 0, :]
    imag = volt_ref[:, 1, :]
    for peer in range(peers):
        start = (peer % split) * part
        out_ref[peer, :, :part] = real[:, start : start + part]
        out_ref[peer, :, part : 2 * part] = imag[:, start : start + part]
        out_ref[peer, :, 2 * part :] = extra


def spread(taps_ref, start, first, count):
    taps = [taps_ref[:, start + k : start + k + 1] for k in range(count)]
    offset = lax.broadcasted_iota(jnp.int32, (first.shape[0], GRID), 1).astype(F32) - first
    out = jnp.zeros_like(offset)
    for k in range(count):
        out = jnp.where(offset == float(k), taps[k], out)
    return out.astype(BF16)


def image_kernel(taps, share, split, scale, row_of, gathered_ref, tables_ref, weight_ref, send_ref,
                 extra_ref, beam_ref, exact_ref, power_ref):
    stations = gathered_ref.shape[0]
    samples = (gathered_ref.shape[1] - LANES) // 2
    peers = send_ref.shape[0] // split
    per_peer = weight_ref.shape[1] // peers
    row = row_of()

    both = gathered_ref[:, : 2 * samples]
    real = gathered_ref[:, :samples]
    imag = gathered_ref[:, samples : 2 * samples]
    outer = (((1,), (1,)), ((), ()))
    corr_real = lax.dot_general(both, both, outer, preferred_element_type=F32)
    corr_imag = lax.dot_general(imag, real, outer, preferred_element_type=F32)
    corr_imag -= lax.dot_general(real, imag, outer, preferred_element_type=F32)
    corr_real = corr_real.astype(BF16)
    corr_both = jnp.concatenate([corr_real, (2.0 * corr_imag).astype(BF16)], axis=1)

    extra_ref[...] = gathered_ref[:, 2 * samples :].astype(F32)
    first_row = extra_ref[:, 4 * taps : 4 * taps + 1]
    first_col = extra_ref[:, 4 * taps + 1 : 4 * taps + 2]
    high = jnp.concatenate(
        [spread(extra_ref, 0, first_row, taps), spread(extra_ref, taps, first_col, taps)], axis=0
    )
    low = jnp.concatenate(
        [spread(extra_ref, 2 * taps, first_row, taps), spread(extra_ref, 3 * taps, first_col, taps)],
        axis=0,
    )
    table_high = tables_ref[:, : 2 * GRID]
    table_low = tables_ref[:, 2 * GRID :]
    response = (
        jnp.dot(high, table_high, preferred_element_type=F32)
        + jnp.dot(high, table_low, preferred_element_type=F32)
        + jnp.dot(low, table_high, preferred_element_type=F32)
    )
    row_real = response[:stations, :GRID]
    row_imag = response[:stations, GRID:]
    first = row // split * (split * share)
    upper = first >= LANES
    turn = lax.rem(2 * LANES - first, LANES)
    column = response[stations:]
    col_real = pltpu.roll(
        jnp.where(upper, column[:, LANES : 2 * LANES], column[:, :LANES]), turn, 1
    )
    col_imag = pltpu.roll(
        jnp.where(upper, column[:, 3 * LANES :], column[:, 2 * LANES : 3 * LANES]), turn, 1
    )

    for m in range(share * split):
        c_real = col_real[:, m : m + 1]
        c_imag = col_imag[:, m : m + 1]
        beam_real = c_real * row_real - c_imag * row_imag
        beam_imag = c_real * row_imag + c_imag * row_real
        exact_ref[m, 0] = beam_real
        exact_ref[m, 1] = beam_imag
        beam_ref[m, :stations] = beam_imag.astype(BF16)
        beam_ref[m, stations:] = beam_real.astype(BF16)
        sum_real = jnp.dot(corr_real, beam_ref[m, stations:], preferred_element_type=F32)
        sum_imag = jnp.dot(corr_both, beam_ref[m], preferred_element_type=F32)
        total = exact_ref[m, 0] * sum_real + exact_ref[m, 1] * sum_imag
        power_ref[m : m + 1, :] = jnp.sum(total, axis=0, keepdims=True) * scale
    weights = weight_ref[...]
    for peer in range(peers):
        own = weights[:, peer * per_peer : (peer + 1) * per_peer]
        own = jnp.concatenate([own, jnp.zeros((1, LANES - per_peer), F32)], axis=1)
        for side in range(split):
            block = peer * split + side
            for m in range(share):
                column = side * share + m
                send_ref[block, :, m * GRID : (m + 1) * GRID] = power_ref[column : column + 1, :]
            send_ref[block, :, share * GRID :] = own


def finish_kernel(split, channel_of, parts_ref, power_ref, maps_ref):
    share = power_ref.shape[0]
    per_peer = maps_ref.shape[0] // share
    channel = channel_of()
    blocks = parts_ref.shape[0]
    parts = parts_ref[:, 0, :]
    source = lax.broadcasted_iota(jnp.int32, (blocks, 1), 0) // split
    mask = jnp.where(source == channel, 1.0, 0.0)
    weights = parts[:, share * GRID :]
    factors = [mask] + [weights[:, q : q + 1] for q in range(per_peer)]
    for m in range(share):
        block = parts[:, m * GRID : (m + 1) * GRID]
        power_ref[m : m + 1, :] = jnp.sum(block * factors[0], axis=0, keepdims=True)
        for q in range(per_peer):
            place = q * share + m
            maps_ref[place : place + 1, :] = jnp.sum(block * factors[1 + q], axis=0, keepdims=True)


def vmem():
    return pl.BlockSpec(memory_space=pltpu.VMEM)


def packed(volt, kern, foot, gain, peers, split):
    stations, _, samples = volt.shape
    inputs = [pltpu.with_memory_space_constraint(x, pltpu.HBM) for x in (volt, kern, foot, gain)]
    return pl.pallas_call(
        functools.partial(pack_kernel, peers, split),
        out_shape=(
            jax.ShapeDtypeStruct((peers, stations, 2 * samples // split + LANES), BF16),
            jax.ShapeDtypeStruct(gain.shape, F32),
        ),
        in_specs=[pl.BlockSpec(memory_space=pltpu.HBM)] * 4,
        out_specs=(vmem(), vmem()),
        scratch_shapes=[
            pltpu.VMEM((LANES, LANES), F32),
            pltpu.VMEM(volt.shape, volt.dtype),
            pltpu.VMEM(kern.shape, kern.dtype),
            pltpu.VMEM(foot.shape, foot.dtype),
            pltpu.SemaphoreType.DMA((4,)),
        ],
        compiler_params=pltpu.CompilerParams(vmem_limit_bytes=8 << 20),
        name="pack",
    )(*inputs)


def imaged(gathered, tables, weight, peers, taps, share, split, scale, row_of, interpret=False):
    stations = gathered.shape[0]
    columns = share * split
    return pl.pallas_call(
        functools.partial(image_kernel, taps, share, split, scale, row_of),
        out_shape=jax.ShapeDtypeStruct((peers * split, 1, share * GRID + LANES), F32),
        in_specs=[vmem()] * 3,
        out_specs=vmem(),
        scratch_shapes=[
            pltpu.VMEM((stations, LANES), F32),
            pltpu.VMEM((columns, 2 * stations, GRID), BF16),
            pltpu.VMEM((columns, 2, stations, GRID), F32),
            pltpu.VMEM((columns, GRID), F32),
        ],
        compiler_params=pltpu.CompilerParams(vmem_limit_bytes=32 << 20),
        name="image",
        interpret=interpret,
    )(gathered, tables, weight)


def finished(parts, share, per_peer, split, channel_of, interpret=False):
    return pl.pallas_call(
        functools.partial(finish_kernel, split, channel_of),
        out_shape=(
            jax.ShapeDtypeStruct((share, GRID), F32),
            jax.ShapeDtypeStruct((per_peer * share, GRID), F32),
        ),
        in_specs=[vmem()],
        out_specs=(vmem(), vmem()),
        compiler_params=pltpu.CompilerParams(vmem_limit_bytes=8 << 20),
        name="finish",
        interpret=interpret,
    )(parts)


def on_device(tables, voltages, kernels, footprint, cal_weight):
    local_stations, _, local_channels, samples = voltages.shape
    rows = lax.axis_size("row")
    channels = lax.axis_size("chan")
    share = GRID // rows
    taps = kernels.shape[2]
    station_count = local_stations * rows
    scale = 1.0 / (2.0 * samples * station_count * taps * taps)
    volt = voltages.reshape(local_stations, 2, samples)
    kern = jnp.transpose(kernels, (1, 2, 0))
    send, weight = packed(volt, kern, footprint.T, cal_weight.T, rows, SPLIT)
    gathered = lax.all_to_all(send, "row", 0, 0, tiled=True)
    gathered = gathered.reshape(station_count, -1)
    weighted = imaged(
        gathered, tables, weight, channels, taps, share, SPLIT, scale,
        lambda: lax.axis_index("row"),
    )
    groups = [
        [c * rows + first + side for c in range(channels) for side in range(SPLIT)]
        for first in range(0, rows, SPLIT)
    ]
    parts = lax.all_to_all(
        weighted, ("chan", "row"), 0, 0, axis_index_groups=groups, tiled=True
    )
    power, maps = finished(parts, share, weight.shape[1] // channels, SPLIT, lambda: lax.axis_index("chan"))
    maps = maps.reshape(-1, share, GRID)
    return jnp.transpose(power[None], (0, 2, 1)), jnp.transpose(maps, (0, 2, 1))


def solution(mesh):
    specs = (P("row", None, "chan", None), P("row", None, None), P("row", None), P(None, "chan"))
    tables = transform_tables()
    return jax.shard_map(
        lambda *args: on_device(jnp.asarray(tables), *args),
        mesh=mesh,
        in_specs=specs,
        out_specs=(P("chan", None, "row"), P("chan", None, "row")),
        check_vma=False,
    )
```

```python
import functools
import math

import jax
import jax.numpy as jnp
import numpy as np
from jax import lax
from jax.experimental import pallas as pl
from jax.experimental.pallas import tpu as pltpu
from jax.sharding import PartitionSpec as P

GRID = 256
LANES = 128
SPLIT = 2
GROUP = 2
BF16 = jnp.bfloat16
F32 = jnp.float32


def transform_tables():
    index = np.arange(GRID)
    angles = (index[:, None] * index[None, :] % GRID) * (2.0 * math.pi / GRID)
    exact = np.concatenate([np.cos(angles), np.sin(angles)], axis=0).astype(np.float32)
    high = exact.astype(BF16)
    low = (exact - high.astype(np.float32)).astype(BF16)
    return np.concatenate([high, low], axis=1)


def rounded(values):
    return values.astype(BF16).astype(F32)


def pack_kernel(peers, split, volt_hbm, kern_hbm, foot_hbm, gain_hbm, out_ref, weight_ref,
                turn_ref, volt_ref, kern_ref, foot_ref, sems):
    pairs = ((kern_hbm, kern_ref), (foot_hbm, foot_ref), (gain_hbm, weight_ref), (volt_hbm, volt_ref))
    copies = [pltpu.make_async_copy(*pair, sems.at[i]) for i, pair in enumerate(pairs)]
    for copy in copies:
        copy.start()
    stations, _, samples = volt_ref.shape
    part = samples // split
    taps = kern_ref.shape[1]
    turn_ref[...] = jnp.zeros_like(turn_ref)
    for copy in copies:
        copy.wait()
    for axis in range(2):
        values = kern_ref[axis]
        high = rounded(values)
        turn_ref[axis * taps : (axis + 1) * taps, :stations] = high
        turn_ref[(2 + axis) * taps : (3 + axis) * taps, :stations] = values - high
    turn_ref[4 * taps : 4 * taps + 2, :stations] = foot_ref[...].astype(F32)
    extra = turn_ref[...].T[:stations].astype(BF16)
    real = volt_ref[:, 0, :]
    imag = volt_ref[:, 1, :]
    for peer in range(peers):
        start = (peer % split) * part
        out_ref[peer, :, :part] = real[:, start : start + part]
        out_ref[peer, :, part : 2 * part] = imag[:, start : start + part]
        out_ref[peer, :, 2 * part :] = extra


def spread(first, high, low):
    offset = lax.broadcasted_iota(jnp.int32, (GRID, first.shape[1]), 0).astype(F32) - first
    offset = offset.astype(BF16)
    high, low = high.astype(BF16), low.astype(BF16)
    out_high = jnp.zeros_like(offset)
    out_low = jnp.zeros_like(offset)
    for k in range(high.shape[0]):
        hit = offset == jnp.asarray(k, BF16)
        out_high = jnp.where(hit, high[k : k + 1], out_high)
        out_low = jnp.where(hit, low[k : k + 1], out_low)
    return out_high, out_low


def respond(table, high, low):
    return (
        jnp.dot(table[:, :GRID], high, preferred_element_type=F32)
        + jnp.dot(table[:, GRID:], high, preferred_element_type=F32)
        + jnp.dot(table[:, :GRID], low, preferred_element_type=F32)
    )


def image_kernel(taps, share, split, scale, row_of, gathered_ref, tables_ref, weight_ref, send_ref,
                 corr_ref, rows_ref, beam_a, beam_b, exact_a, exact_b, column_ref):
    stations = gathered_ref.shape[0]
    samples = (gathered_ref.shape[1] - LANES) // 2
    peers = send_ref.shape[0] // split
    per_peer = weight_ref.shape[1] // peers
    columns = share * split
    row = row_of()

    both = gathered_ref[:, : 2 * samples]
    real = gathered_ref[:, :samples]
    imag = gathered_ref[:, samples : 2 * samples]
    outer = (((1,), (1,)), ((), ()))
    corr_ref[stations:] = lax.dot_general(both, both, outer, preferred_element_type=F32).astype(BF16)
    turned = lax.dot_general(real, imag, outer, preferred_element_type=F32)
    turned -= lax.dot_general(imag, real, outer, preferred_element_type=F32)
    corr_ref[:stations] = (2.0 * turned).astype(BF16)

    extra = gathered_ref[:, 2 * samples :].astype(F32).T
    high, low, first = extra[: 2 * taps], extra[2 * taps : 4 * taps], extra[4 * taps : 4 * taps + 2]
    row_high, row_low = spread(first[:1], high[:taps], low[:taps])
    col_high, col_low = spread(first[1:], high[taps:], low[taps:])
    rows_ref[...] = respond(tables_ref[...], row_high, row_low)
    base = pl.multiple_of(row // split * columns, columns)
    column_cos = respond(tables_ref[pl.ds(base, columns), :], col_high, col_low)
    column_sin = respond(tables_ref[pl.ds(GRID + base, columns), :], col_high, col_low)

    slots = ((beam_a, exact_a), (beam_b, exact_b))

    group = beam_a.shape[0] // GRID

    def build(step):
        beam, exact = slots[step % 2]
        r_real, r_imag = rows_ref[:GRID], rows_ref[GRID:]
        for j in range(group):
            m = step * group + j
            lines = slice(j * GRID, (j + 1) * GRID)
            c_real, c_imag = column_cos[m : m + 1], column_sin[m : m + 1]
            beam_real = c_real * r_real - c_imag * r_imag
            beam_imag = c_real * r_imag + c_imag * r_real
            exact[0, lines] = beam_real
            exact[1, lines] = beam_imag
            beam[lines, :stations] = beam_real.astype(BF16)
            beam[lines, stations:] = beam_imag.astype(BF16)

    build(0)
    steps = columns // group
    for step in range(steps):
        beam, exact = slots[step % 2]
        sum_real = jnp.dot(beam[:, :stations], corr_ref[stations:], preferred_element_type=F32)
        sum_imag = jnp.dot(beam[...], corr_ref[...], preferred_element_type=F32)
        if step + 1 < steps:
            build(step + 1)
        total = exact[0] * sum_real + exact[1] * sum_imag
        power = jnp.sum(total, axis=1, keepdims=True) * scale
        for j in range(group):
            m = step * group + j
            column_ref[:, m : m + 1] = power[j * GRID : (j + 1) * GRID]
    power = column_ref[...].T
    weights = weight_ref[...]
    for peer in range(peers):
        own = weights[:, peer * per_peer : (peer + 1) * per_peer]
        own = jnp.concatenate([own, jnp.zeros((1, LANES - per_peer), F32)], axis=1)
        for side in range(split):
            block = peer * split + side
            for m in range(share):
                column = side * share + m
                send_ref[block, :, m * GRID : (m + 1) * GRID] = power[column : column + 1, :]
            send_ref[block, :, share * GRID :] = own


def finish_kernel(split, channel_of, parts_ref, power_ref, maps_ref):
    share = power_ref.shape[0]
    per_peer = maps_ref.shape[0] // share
    channel = channel_of()
    blocks = parts_ref.shape[0]
    parts = parts_ref[:, 0, :]
    source = lax.broadcasted_iota(jnp.int32, (blocks, 1), 0) // split
    mask = jnp.where(source == channel, 1.0, 0.0)
    weights = parts[:, share * GRID :]
    factors = [mask] + [weights[:, q : q + 1] for q in range(per_peer)]
    for m in range(share):
        block = parts[:, m * GRID : (m + 1) * GRID]
        power_ref[m : m + 1, :] = jnp.sum(block * factors[0], axis=0, keepdims=True)
        for q in range(per_peer):
            place = q * share + m
            maps_ref[place : place + 1, :] = jnp.sum(block * factors[1 + q], axis=0, keepdims=True)


def vmem():
    return pl.BlockSpec(memory_space=pltpu.VMEM)


def packed(volt, kern, foot, gain, peers, split):
    stations, _, samples = volt.shape
    inputs = [pltpu.with_memory_space_constraint(x, pltpu.HBM) for x in (volt, kern, foot, gain)]
    return pl.pallas_call(
        functools.partial(pack_kernel, peers, split),
        out_shape=(
            jax.ShapeDtypeStruct((peers, stations, 2 * samples // split + LANES), BF16),
            jax.ShapeDtypeStruct(gain.shape, F32),
        ),
        in_specs=[pl.BlockSpec(memory_space=pltpu.HBM)] * 4,
        out_specs=(vmem(), vmem()),
        scratch_shapes=[
            pltpu.VMEM((LANES, LANES), F32),
            pltpu.VMEM(volt.shape, volt.dtype),
            pltpu.VMEM(kern.shape, kern.dtype),
            pltpu.VMEM(foot.shape, foot.dtype),
            pltpu.SemaphoreType.DMA((4,)),
        ],
        compiler_params=pltpu.CompilerParams(vmem_limit_bytes=8 << 20),
        name="pack",
    )(*inputs)


def imaged(gathered, tables, weight, peers, taps, share, split, scale, row_of, interpret=False):
    stations = gathered.shape[0]
    return pl.pallas_call(
        functools.partial(image_kernel, taps, share, split, scale, row_of),
        out_shape=jax.ShapeDtypeStruct((peers * split, 1, share * GRID + LANES), F32),
        in_specs=[vmem()] * 3,
        out_specs=vmem(),
        scratch_shapes=[
            pltpu.VMEM((2 * stations, stations), BF16),
            pltpu.VMEM((2 * GRID, stations), F32),
            pltpu.VMEM((GROUP * GRID, 2 * stations), BF16),
            pltpu.VMEM((GROUP * GRID, 2 * stations), BF16),
            pltpu.VMEM((2, GROUP * GRID, stations), F32),
            pltpu.VMEM((2, GROUP * GRID, stations), F32),
            pltpu.VMEM((GRID, LANES), F32),
        ],
        compiler_params=pltpu.CompilerParams(vmem_limit_bytes=32 << 20),
        name="image",
        interpret=interpret,
    )(gathered, tables, weight)


def finished(parts, share, per_peer, split, channel_of, interpret=False):
    return pl.pallas_call(
        functools.partial(finish_kernel, split, channel_of),
        out_shape=(
            jax.ShapeDtypeStruct((share, GRID), F32),
            jax.ShapeDtypeStruct((per_peer * share, GRID), F32),
        ),
        in_specs=[vmem()],
        out_specs=(vmem(), vmem()),
        compiler_params=pltpu.CompilerParams(vmem_limit_bytes=8 << 20),
        name="finish",
        interpret=interpret,
    )(parts)


def on_device(tables, voltages, kernels, footprint, cal_weight):
    local_stations, _, local_channels, samples = voltages.shape
    rows = lax.axis_size("row")
    channels = lax.axis_size("chan")
    share = GRID // rows
    taps = kernels.shape[2]
    station_count = local_stations * rows
    scale = 1.0 / (2.0 * samples * station_count * taps * taps)
    volt = voltages.reshape(local_stations, 2, samples)
    kern = jnp.transpose(kernels, (1, 2, 0))
    send, weight = packed(volt, kern, footprint.T, cal_weight.T, rows, SPLIT)
    gathered = lax.all_to_all(send, "row", 0, 0, tiled=True)
    gathered = gathered.reshape(station_count, -1)
    weighted = imaged(
        gathered, tables, weight, channels, taps, share, SPLIT, scale,
        lambda: lax.axis_index("row"),
    )
    groups = [
        [c * rows + first + side for c in range(channels) for side in range(SPLIT)]
        for first in range(0, rows, SPLIT)
    ]
    parts = lax.all_to_all(
        weighted, ("chan", "row"), 0, 0, axis_index_groups=groups, tiled=True
    )
    power, maps = finished(parts, share, weight.shape[1] // channels, SPLIT, lambda: lax.axis_index("chan"))
    maps = maps.reshape(-1, share, GRID)
    return jnp.transpose(power[None], (0, 2, 1)), jnp.transpose(maps, (0, 2, 1))


def solution(mesh):
    specs = (P("row", None, "chan", None), P("row", None, None), P("row", None), P(None, "chan"))
    tables = transform_tables()
    return jax.shard_map(
        lambda *args: on_device(jnp.asarray(tables), *args),
        mesh=mesh,
        in_specs=specs,
        out_specs=(P("chan", None, "row"), P("chan", None, "row")),
        check_vma=False,
    )
```

```python
import functools
import math

import jax
import jax.numpy as jnp
import numpy as np
from jax import lax
from jax.experimental import pallas as pl
from jax.experimental.pallas import tpu as pltpu
from jax.sharding import PartitionSpec as P

GRID = 256
LANES = 128
DEPTH = 8
SPLIT_X = 2
SPLIT_Z = 2
SPLIT = SPLIT_X * SPLIT_Z
GROUP = 2
BF16 = jnp.bfloat16
F32 = jnp.float32


def transform_tables():
    index = np.arange(GRID)
    angles = (index[:, None] * index[None, :] % GRID) * (2.0 * math.pi / GRID)
    exact = np.concatenate([np.cos(angles), np.sin(angles)], axis=0).astype(np.float32)
    high = exact.astype(BF16)
    low = (exact - high.astype(np.float32)).astype(BF16)
    return np.concatenate([high, low], axis=1)


def side_of(row):
    return row // DEPTH % SPLIT_X * SPLIT_Z + row % DEPTH % SPLIT_Z


def neighbours(row):
    x, z = row // DEPTH // SPLIT_X * SPLIT_X, row % DEPTH // SPLIT_Z * SPLIT_Z
    return [(x + i) * DEPTH + z + j for i in range(SPLIT_X) for j in range(SPLIT_Z)]


def rounded(values):
    return values.astype(BF16).astype(F32)


def pack_kernel(peers, split, volt_hbm, kern_hbm, foot_hbm, gain_hbm, out_ref, weight_ref,
                turn_ref, volt_ref, kern_ref, foot_ref, sems):
    pairs = ((kern_hbm, kern_ref), (foot_hbm, foot_ref), (gain_hbm, weight_ref), (volt_hbm, volt_ref))
    copies = [pltpu.make_async_copy(*pair, sems.at[i]) for i, pair in enumerate(pairs)]
    for copy in copies:
        copy.start()
    stations, _, samples = volt_ref.shape
    part = samples // split
    taps = kern_ref.shape[1]
    turn_ref[...] = jnp.zeros_like(turn_ref)
    for copy in copies:
        copy.wait()
    for axis in range(2):
        values = kern_ref[axis]
        high = rounded(values)
        turn_ref[axis * taps : (axis + 1) * taps, :stations] = high
        turn_ref[(2 + axis) * taps : (3 + axis) * taps, :stations] = values - high
    turn_ref[4 * taps : 4 * taps + 2, :stations] = foot_ref[...].astype(F32)
    extra = turn_ref[...].T[:stations].astype(BF16)
    real = volt_ref[:, 0, :]
    imag = volt_ref[:, 1, :]
    for peer in range(peers):
        start = side_of(peer) * part
        out_ref[peer, :, :part] = real[:, start : start + part]
        out_ref[peer, :, part : 2 * part] = imag[:, start : start + part]
        out_ref[peer, :, 2 * part :] = extra


def spread(first, high, low):
    offset = lax.broadcasted_iota(jnp.int32, (GRID, first.shape[1]), 0).astype(F32) - first
    offset = offset.astype(BF16)
    high, low = high.astype(BF16), low.astype(BF16)
    out_high = jnp.zeros_like(offset)
    out_low = jnp.zeros_like(offset)
    for k in range(high.shape[0]):
        hit = offset == jnp.asarray(k, BF16)
        out_high = jnp.where(hit, high[k : k + 1], out_high)
        out_low = jnp.where(hit, low[k : k + 1], out_low)
    return out_high, out_low


def respond(table, high, low):
    return (
        jnp.dot(table[:, :GRID], high, preferred_element_type=F32)
        + jnp.dot(table[:, GRID:], high, preferred_element_type=F32)
        + jnp.dot(table[:, :GRID], low, preferred_element_type=F32)
    )


def image_kernel(taps, share, split, scale, row_of, gathered_ref, tables_ref, weight_ref, send_ref,
                 corr_ref, rows_ref, beam_a, beam_b, exact_a, exact_b, column_ref):
    stations = gathered_ref.shape[0]
    samples = (gathered_ref.shape[1] - LANES) // 2
    peers = send_ref.shape[0] // split
    per_peer = weight_ref.shape[1] // peers
    columns = share * split
    row = row_of()

    both = gathered_ref[:, : 2 * samples]
    real = gathered_ref[:, :samples]
    imag = gathered_ref[:, samples : 2 * samples]
    outer = (((1,), (1,)), ((), ()))
    corr_ref[stations:] = lax.dot_general(both, both, outer, preferred_element_type=F32).astype(BF16)
    turned = lax.dot_general(real, imag, outer, preferred_element_type=F32)
    turned -= lax.dot_general(imag, real, outer, preferred_element_type=F32)
    corr_ref[:stations] = (2.0 * turned).astype(BF16)

    extra = gathered_ref[:, 2 * samples :].astype(F32).T
    high, low, first = extra[: 2 * taps], extra[2 * taps : 4 * taps], extra[4 * taps : 4 * taps + 2]
    row_high, row_low = spread(first[:1], high[:taps], low[:taps])
    col_high, col_low = spread(first[1:], high[taps:], low[taps:])
    rows_ref[...] = respond(tables_ref[...], row_high, row_low)
    run = share * SPLIT_Z
    bases = [pl.multiple_of(first * share, run) for first in neighbours(row)[::SPLIT_Z]]
    mine = [tables_ref[pl.ds(part + base, run), :] for part in (0, GRID) for base in bases]
    column = respond(jnp.concatenate(mine, axis=0), col_high, col_low)
    column_cos, column_sin = column[:columns], column[columns:]

    slots = ((beam_a, exact_a), (beam_b, exact_b))

    group = beam_a.shape[0] // GRID

    def build(step):
        beam, exact = slots[step % 2]
        r_real, r_imag = rows_ref[:GRID], rows_ref[GRID:]
        for j in range(group):
            m = step * group + j
            lines = slice(j * GRID, (j + 1) * GRID)
            c_real, c_imag = column_cos[m : m + 1], column_sin[m : m + 1]
            beam_real = c_real * r_real - c_imag * r_imag
            beam_imag = c_real * r_imag + c_imag * r_real
            exact[0, lines] = beam_real
            exact[1, lines] = beam_imag
            beam[lines, :stations] = beam_real.astype(BF16)
            beam[lines, stations:] = beam_imag.astype(BF16)

    build(0)
    steps = columns // group
    for step in range(steps):
        beam, exact = slots[step % 2]
        sum_real = jnp.dot(beam[:, :stations], corr_ref[stations:], preferred_element_type=F32)
        product = exact[0] * sum_real
        total = product[:, :LANES] + product[:, LANES:]
        sum_imag = jnp.dot(beam[...], corr_ref[...], preferred_element_type=F32)
        if step + 1 < steps:
            build(step + 1)
        product = exact[1] * sum_imag
        total += product[:, :LANES] + product[:, LANES:]
        power = jnp.sum(total, axis=1, keepdims=True) * scale
        for j in range(group):
            m = step * group + j
            column_ref[:, m : m + 1] = power[j * GRID : (j + 1) * GRID]
    power = column_ref[...].T
    weights = weight_ref[...]
    for peer in range(peers):
        own = weights[:, peer * per_peer : (peer + 1) * per_peer]
        own = jnp.concatenate([own, jnp.zeros((1, LANES - per_peer), F32)], axis=1)
        for side in range(split):
            block = peer * split + side
            for m in range(share):
                column = side * share + m
                send_ref[block, :, m * GRID : (m + 1) * GRID] = power[column : column + 1, :]
            send_ref[block, :, share * GRID :] = own


def finish_kernel(split, channel_of, parts_ref, power_ref, maps_ref):
    share = power_ref.shape[0]
    per_peer = maps_ref.shape[0] // share
    channel = channel_of()
    blocks = parts_ref.shape[0]
    parts = parts_ref[:, 0, :]
    source = lax.broadcasted_iota(jnp.int32, (blocks, 1), 0) // split
    mask = jnp.where(source == channel, 1.0, 0.0)
    weights = parts[:, share * GRID :]
    factors = [mask] + [weights[:, q : q + 1] for q in range(per_peer)]
    for m in range(share):
        block = parts[:, m * GRID : (m + 1) * GRID]
        power_ref[m : m + 1, :] = jnp.sum(block * factors[0], axis=0, keepdims=True)
        for q in range(per_peer):
            place = q * share + m
            maps_ref[place : place + 1, :] = jnp.sum(block * factors[1 + q], axis=0, keepdims=True)


def vmem():
    return pl.BlockSpec(memory_space=pltpu.VMEM)


def packed(volt, kern, foot, gain, peers, split):
    stations, _, samples = volt.shape
    inputs = [pltpu.with_memory_space_constraint(x, pltpu.HBM) for x in (volt, kern, foot, gain)]
    return pl.pallas_call(
        functools.partial(pack_kernel, peers, split),
        out_shape=(
            jax.ShapeDtypeStruct((peers, stations, 2 * samples // split + LANES), BF16),
            jax.ShapeDtypeStruct(gain.shape, F32),
        ),
        in_specs=[pl.BlockSpec(memory_space=pltpu.HBM)] * 4,
        out_specs=(vmem(), vmem()),
        scratch_shapes=[
            pltpu.VMEM((LANES, LANES), F32),
            pltpu.VMEM(volt.shape, volt.dtype),
            pltpu.VMEM(kern.shape, kern.dtype),
            pltpu.VMEM(foot.shape, foot.dtype),
            pltpu.SemaphoreType.DMA((4,)),
        ],
        compiler_params=pltpu.CompilerParams(vmem_limit_bytes=8 << 20),
        name="pack",
    )(*inputs)


def imaged(gathered, tables, weight, peers, taps, share, split, scale, row_of, interpret=False):
    stations = gathered.shape[0]
    return pl.pallas_call(
        functools.partial(image_kernel, taps, share, split, scale, row_of),
        out_shape=jax.ShapeDtypeStruct((peers * split, 1, share * GRID + LANES), F32),
        in_specs=[vmem()] * 3,
        out_specs=vmem(),
        scratch_shapes=[
            pltpu.VMEM((2 * stations, stations), BF16),
            pltpu.VMEM((2 * GRID, stations), F32),
            pltpu.VMEM((GROUP * GRID, 2 * stations), BF16),
            pltpu.VMEM((GROUP * GRID, 2 * stations), BF16),
            pltpu.VMEM((2, GROUP * GRID, stations), F32),
            pltpu.VMEM((2, GROUP * GRID, stations), F32),
            pltpu.VMEM((GRID, LANES), F32),
        ],
        compiler_params=pltpu.CompilerParams(vmem_limit_bytes=32 << 20),
        name="image",
        interpret=interpret,
    )(gathered, tables, weight)


def finished(parts, share, per_peer, split, channel_of, interpret=False):
    return pl.pallas_call(
        functools.partial(finish_kernel, split, channel_of),
        out_shape=(
            jax.ShapeDtypeStruct((share, GRID), F32),
            jax.ShapeDtypeStruct((per_peer * share, GRID), F32),
        ),
        in_specs=[vmem()],
        out_specs=(vmem(), vmem()),
        compiler_params=pltpu.CompilerParams(vmem_limit_bytes=8 << 20),
        name="finish",
        interpret=interpret,
    )(parts)


def on_device(tables, voltages, kernels, footprint, cal_weight):
    local_stations, _, local_channels, samples = voltages.shape
    rows = lax.axis_size("row")
    channels = lax.axis_size("chan")
    share = GRID // rows
    taps = kernels.shape[2]
    station_count = local_stations * rows
    scale = 1.0 / (2.0 * samples * station_count * taps * taps)
    volt = voltages.reshape(local_stations, 2, samples)
    kern = jnp.transpose(kernels, (1, 2, 0))
    send, weight = packed(volt, kern, footprint.T, cal_weight.T, rows, SPLIT)
    gathered = lax.all_to_all(send, "row", 0, 0, tiled=True)
    gathered = gathered.reshape(station_count, -1)
    weighted = imaged(
        gathered, tables, weight, channels, taps, share, SPLIT, scale,
        lambda: lax.axis_index("row"),
    )
    groups = [
        [c * rows + near for c in range(channels) for near in neighbours(row)]
        for row in range(rows)
        if side_of(row) == 0
    ]
    parts = lax.all_to_all(
        weighted, ("chan", "row"), 0, 0, axis_index_groups=groups, tiled=True
    )
    power, maps = finished(parts, share, weight.shape[1] // channels, SPLIT, lambda: lax.axis_index("chan"))
    maps = maps.reshape(-1, share, GRID)
    return jnp.transpose(power[None], (0, 2, 1)), jnp.transpose(maps, (0, 2, 1))


def solution(mesh):
    specs = (P("row", None, "chan", None), P("row", None, None), P("row", None), P(None, "chan"))
    tables = transform_tables()
    return jax.shard_map(
        lambda *args: on_device(jnp.asarray(tables), *args),
        mesh=mesh,
        in_specs=specs,
        out_specs=(P("chan", None, "row"), P("chan", None, "row")),
        check_vma=False,
    )
```

```python
import functools
import math

import jax
import jax.numpy as jnp
import numpy as np
from jax import lax
from jax.experimental import pallas as pl
from jax.experimental.pallas import tpu as pltpu
from jax.sharding import PartitionSpec as P

GRID = 256
LANES = 128
DEPTH = 8
SPLIT_X = 2
SPLIT_Z = 2
SPLIT = SPLIT_X * SPLIT_Z
GROUP = 2
BF16 = jnp.bfloat16
F32 = jnp.float32


def transform_tables():
    index = np.arange(GRID)
    angles = (index[:, None] * index[None, :] % GRID) * (2.0 * math.pi / GRID)
    exact = np.concatenate([np.cos(angles), np.sin(angles)], axis=0).astype(np.float32)
    high = exact.astype(BF16)
    low = (exact - high.astype(np.float32)).astype(BF16)
    return np.concatenate([high, low], axis=1)


def side_of(row):
    return row // DEPTH % SPLIT_X * SPLIT_Z + row % DEPTH % SPLIT_Z


def neighbours(row):
    x, z = row // DEPTH // SPLIT_X * SPLIT_X, row % DEPTH // SPLIT_Z * SPLIT_Z
    return [(x + i) * DEPTH + z + j for i in range(SPLIT_X) for j in range(SPLIT_Z)]


def rounded(values):
    return values.astype(BF16).astype(F32)


def pack_kernel(peers, split, volt_hbm, kern_hbm, foot_hbm, gain_hbm, out_ref, weight_ref,
                turn_ref, volt_ref, kern_ref, foot_ref, sems):
    pairs = ((kern_hbm, kern_ref), (foot_hbm, foot_ref), (gain_hbm, weight_ref), (volt_hbm, volt_ref))
    copies = [pltpu.make_async_copy(*pair, sems.at[i]) for i, pair in enumerate(pairs)]
    for copy in copies:
        copy.start()
    stations, _, samples = volt_ref.shape
    part = samples // split
    taps = kern_ref.shape[1]
    turn_ref[...] = jnp.zeros_like(turn_ref)
    for copy in copies:
        copy.wait()
    for axis in range(2):
        values = kern_ref[axis]
        high = rounded(values)
        turn_ref[axis * taps : (axis + 1) * taps, :stations] = high
        turn_ref[(2 + axis) * taps : (3 + axis) * taps, :stations] = values - high
    turn_ref[4 * taps : 4 * taps + 2, :stations] = foot_ref[...].astype(F32)
    extra = turn_ref[...].T[:stations].astype(BF16)
    real = volt_ref[:, 0, :]
    imag = volt_ref[:, 1, :]
    for peer in range(peers):
        start = side_of(peer) * part
        out_ref[peer, :, :part] = real[:, start : start + part]
        out_ref[peer, :, part : 2 * part] = imag[:, start : start + part]
        out_ref[peer, :, 2 * part :] = extra


def spread(first, high, low):
    offset = lax.broadcasted_iota(jnp.int32, (GRID, first.shape[1]), 0).astype(F32) - first
    offset = offset.astype(BF16)
    high, low = high.astype(BF16), low.astype(BF16)
    out_high = jnp.zeros_like(offset)
    out_low = jnp.zeros_like(offset)
    for k in range(high.shape[0]):
        hit = offset == jnp.asarray(k, BF16)
        out_high = jnp.where(hit, high[k : k + 1], out_high)
        out_low = jnp.where(hit, low[k : k + 1], out_low)
    return out_high, out_low


def respond(table, high, low):
    return (
        jnp.dot(table[:, :GRID], high, preferred_element_type=F32)
        + jnp.dot(table[:, GRID:], high, preferred_element_type=F32)
        + jnp.dot(table[:, :GRID], low, preferred_element_type=F32)
    )


def image_kernel(taps, share, split, scale, row_of, gathered_ref, tables_ref, weight_ref, send_ref,
                 corr_ref, rows_ref, beam_a, beam_b, exact_a, exact_b, column_ref):
    stations = gathered_ref.shape[0]
    samples = (gathered_ref.shape[1] - LANES) // 2
    depth = GRID // LANES * share + 1
    peers = send_ref.shape[0] // (depth * split)
    per_peer = weight_ref.shape[1] // peers
    columns = share * split
    row = row_of()

    both = gathered_ref[:, : 2 * samples]
    real = gathered_ref[:, :samples]
    imag = gathered_ref[:, samples : 2 * samples]
    outer = (((1,), (1,)), ((), ()))
    corr_ref[stations:] = lax.dot_general(both, both, outer, preferred_element_type=F32).astype(BF16)
    turned = lax.dot_general(real, imag, outer, preferred_element_type=F32)
    turned -= lax.dot_general(imag, real, outer, preferred_element_type=F32)
    corr_ref[:stations] = (2.0 * turned).astype(BF16)

    extra = gathered_ref[:, 2 * samples :].astype(F32).T
    high, low, first = extra[: 2 * taps], extra[2 * taps : 4 * taps], extra[4 * taps : 4 * taps + 2]
    row_high, row_low = spread(first[:1], high[:taps], low[:taps])
    col_high, col_low = spread(first[1:], high[taps:], low[taps:])
    rows_ref[...] = respond(tables_ref[...], row_high, row_low)
    run = share * SPLIT_Z
    bases = [pl.multiple_of(first * share, run) for first in neighbours(row)[::SPLIT_Z]]
    mine = [tables_ref[pl.ds(part + base, run), :] for part in (0, GRID) for base in bases]
    column = respond(jnp.concatenate(mine, axis=0), col_high, col_low)
    column_cos, column_sin = column[:columns], column[columns:]

    slots = ((beam_a, exact_a), (beam_b, exact_b))

    group = beam_a.shape[0] // GRID

    def build(step):
        beam, exact = slots[step % 2]
        r_real, r_imag = rows_ref[:GRID], rows_ref[GRID:]
        for j in range(group):
            m = step * group + j
            lines = slice(j * GRID, (j + 1) * GRID)
            c_real, c_imag = column_cos[m : m + 1], column_sin[m : m + 1]
            beam_real = c_real * r_real - c_imag * r_imag
            beam_imag = c_real * r_imag + c_imag * r_real
            exact[0, lines] = beam_real
            exact[1, lines] = beam_imag
            beam[lines, :stations] = beam_real.astype(BF16)
            beam[lines, stations:] = beam_imag.astype(BF16)

    build(0)
    steps = columns // group
    for step in range(steps):
        beam, exact = slots[step % 2]
        sum_real = jnp.dot(beam[:, :stations], corr_ref[stations:], preferred_element_type=F32)
        product = exact[0] * sum_real
        total = product[:, :LANES] + product[:, LANES:]
        sum_imag = jnp.dot(beam[...], corr_ref[...], preferred_element_type=F32)
        if step + 1 < steps:
            build(step + 1)
        product = exact[1] * sum_imag
        total += product[:, :LANES] + product[:, LANES:]
        power = jnp.sum(total, axis=1, keepdims=True) * scale
        for j in range(group):
            m = step * group + j
            column_ref[:, m : m + 1] = power[j * GRID : (j + 1) * GRID]
    power = column_ref[...].T
    weights = weight_ref[...]
    for peer in range(peers):
        own = weights[:, peer * per_peer : (peer + 1) * per_peer]
        own = jnp.concatenate([own, jnp.zeros((1, LANES - per_peer), F32)], axis=1)
        for side in range(split):
            start = (peer * split + side) * depth
            for half in range(GRID // LANES):
                lines = power[side * share : (side + 1) * share, half * LANES : (half + 1) * LANES]
                send_ref[start + half * share : start + (half + 1) * share, :] = lines
            send_ref[start + depth - 1 : start + depth, :] = own


def finish_kernel(split, channel_of, parts_ref, power_ref, maps_ref):
    share = power_ref.shape[0]
    per_peer = maps_ref.shape[0] // share
    halves = GRID // LANES
    depth = halves * share + 1
    channel = channel_of()
    blocks = parts_ref.shape[0] // depth
    power = jnp.zeros((halves * share, LANES), F32)
    maps = [power] * per_peer
    for block in range(blocks):
        start = block * depth
        part = parts_ref[start : start + depth - 1, :]
        weights = parts_ref[start + depth - 1 : start + depth, :]
        power += jnp.where(channel == block // split, part, 0.0)
        for q in range(per_peer):
            maps[q] += part * weights[:, q : q + 1]
    for half in range(halves):
        lanes = slice(half * LANES, (half + 1) * LANES)
        lines = slice(half * share, (half + 1) * share)
        power_ref[:, lanes] = power[lines]
        for q in range(per_peer):
            maps_ref[q * share : (q + 1) * share, lanes] = maps[q][lines]


def vmem():
    return pl.BlockSpec(memory_space=pltpu.VMEM)


def packed(volt, kern, foot, gain, peers, split):
    stations, _, samples = volt.shape
    inputs = [pltpu.with_memory_space_constraint(x, pltpu.HBM) for x in (volt, kern, foot, gain)]
    return pl.pallas_call(
        functools.partial(pack_kernel, peers, split),
        out_shape=(
            jax.ShapeDtypeStruct((peers, stations, 2 * samples // split + LANES), BF16),
            jax.ShapeDtypeStruct(gain.shape, F32),
        ),
        in_specs=[pl.BlockSpec(memory_space=pltpu.HBM)] * 4,
        out_specs=(vmem(), vmem()),
        scratch_shapes=[
            pltpu.VMEM((LANES, LANES), F32),
            pltpu.VMEM(volt.shape, volt.dtype),
            pltpu.VMEM(kern.shape, kern.dtype),
            pltpu.VMEM(foot.shape, foot.dtype),
            pltpu.SemaphoreType.DMA((4,)),
        ],
        compiler_params=pltpu.CompilerParams(vmem_limit_bytes=8 << 20),
        name="pack",
    )(*inputs)


def imaged(gathered, tables, weight, peers, taps, share, split, scale, row_of, interpret=False):
    stations = gathered.shape[0]
    return pl.pallas_call(
        functools.partial(image_kernel, taps, share, split, scale, row_of),
        out_shape=jax.ShapeDtypeStruct((peers * split * (share * GRID // LANES + 1), LANES), F32),
        in_specs=[vmem()] * 3,
        out_specs=vmem(),
        scratch_shapes=[
            pltpu.VMEM((2 * stations, stations), BF16),
            pltpu.VMEM((2 * GRID, stations), F32),
            pltpu.VMEM((GROUP * GRID, 2 * stations), BF16),
            pltpu.VMEM((GROUP * GRID, 2 * stations), BF16),
            pltpu.VMEM((2, GROUP * GRID, stations), F32),
            pltpu.VMEM((2, GROUP * GRID, stations), F32),
            pltpu.VMEM((GRID, LANES), F32),
        ],
        compiler_params=pltpu.CompilerParams(vmem_limit_bytes=32 << 20),
        name="image",
        interpret=interpret,
    )(gathered, tables, weight)


def finished(parts, share, per_peer, split, channel_of, interpret=False):
    return pl.pallas_call(
        functools.partial(finish_kernel, split, channel_of),
        out_shape=(
            jax.ShapeDtypeStruct((share, GRID), F32),
            jax.ShapeDtypeStruct((per_peer * share, GRID), F32),
        ),
        in_specs=[vmem()],
        out_specs=(vmem(), vmem()),
        compiler_params=pltpu.CompilerParams(vmem_limit_bytes=8 << 20),
        name="finish",
        interpret=interpret,
    )(parts)


def on_device(tables, voltages, kernels, footprint, cal_weight):
    local_stations, _, local_channels, samples = voltages.shape
    rows = lax.axis_size("row")
    channels = lax.axis_size("chan")
    share = GRID // rows
    taps = kernels.shape[2]
    station_count = local_stations * rows
    scale = 1.0 / (2.0 * samples * station_count * taps * taps)
    volt = voltages.reshape(local_stations, 2, samples)
    kern = jnp.transpose(kernels, (1, 2, 0))
    send, weight = packed(volt, kern, footprint.T, cal_weight.T, rows, SPLIT)
    gathered = lax.all_to_all(send, "row", 0, 0, tiled=True)
    gathered = gathered.reshape(station_count, -1)
    weighted = imaged(
        gathered, tables, weight, channels, taps, share, SPLIT, scale,
        lambda: lax.axis_index("row"),
    )
    groups = [
        [c * rows + near for c in range(channels) for near in neighbours(row)]
        for row in range(rows)
        if side_of(row) == 0
    ]
    weighted = weighted.reshape(channels * SPLIT, 1, -1)
    parts = lax.all_to_all(
        weighted, ("chan", "row"), 0, 0, axis_index_groups=groups, tiled=True
    )
    parts = parts.reshape(-1, LANES)
    power, maps = finished(parts, share, weight.shape[1] // channels, SPLIT, lambda: lax.axis_index("chan"))
    maps = maps.reshape(-1, share, GRID)
    return jnp.transpose(power[None], (0, 2, 1)), jnp.transpose(maps, (0, 2, 1))


def solution(mesh):
    specs = (P("row", None, "chan", None), P("row", None, None), P("row", None), P(None, "chan"))
    tables = transform_tables()
    return jax.shard_map(
        lambda *args: on_device(jnp.asarray(tables), *args),
        mesh=mesh,
        in_specs=specs,
        out_specs=(P("chan", None, "row"), P("chan", None, "row")),
        check_vma=False,
    )
```

```python
import functools
import math

import jax
import jax.numpy as jnp
import numpy as np
from jax import lax
from jax.experimental import pallas as pl
from jax.experimental.pallas import tpu as pltpu
from jax.sharding import PartitionSpec as P

GRID = 256
LANES = 128
DEPTH = 8
SPLIT_X = 2
SPLIT_Z = 2
SPLIT = SPLIT_X * SPLIT_Z
GROUP = 2
BF16 = jnp.bfloat16
F32 = jnp.float32


def transform_tables():
    index = np.arange(GRID)
    angles = (index[:, None] * index[None, :] % GRID) * (2.0 * math.pi / GRID)
    exact = np.concatenate([np.cos(angles), np.sin(angles)], axis=0).astype(np.float32)
    high = exact.astype(BF16)
    low = (exact - high.astype(np.float32)).astype(BF16)
    return np.concatenate([high, low], axis=1)


def side_of(row):
    return row // DEPTH % SPLIT_X * SPLIT_Z + row % DEPTH % SPLIT_Z


def neighbours(row):
    x, z = row // DEPTH // SPLIT_X * SPLIT_X, row % DEPTH // SPLIT_Z * SPLIT_Z
    return [(x + i) * DEPTH + z + j for i in range(SPLIT_X) for j in range(SPLIT_Z)]


def rounded(values):
    return values.astype(BF16).astype(F32)


def pack_kernel(peers, split, volt_hbm, kern_hbm, foot_hbm, gain_hbm, out_ref, weight_ref,
                turn_ref, volt_ref, kern_ref, foot_ref, sems):
    pairs = ((kern_hbm, kern_ref), (foot_hbm, foot_ref), (gain_hbm, weight_ref), (volt_hbm, volt_ref))
    copies = [pltpu.make_async_copy(*pair, sems.at[i]) for i, pair in enumerate(pairs)]
    for copy in copies:
        copy.start()
    stations, _, samples = volt_ref.shape
    part = samples // split
    taps = kern_ref.shape[1]
    turn_ref[...] = jnp.zeros_like(turn_ref)
    for copy in copies:
        copy.wait()
    for axis in range(2):
        values = kern_ref[axis]
        high = rounded(values)
        turn_ref[axis * taps : (axis + 1) * taps, :stations] = high
        turn_ref[(2 + axis) * taps : (3 + axis) * taps, :stations] = values - high
    turn_ref[4 * taps : 4 * taps + 2, :stations] = foot_ref[...].astype(F32)
    lines = []
    for start, stop in ((0, 4 * taps), (4 * taps, 4 * taps + 2)):
        line = turn_ref[start : start + 1]
        for k in range(start + 1, stop):
            line = line + pltpu.roll(turn_ref[k : k + 1], (k - start) * stations, 1)
        lines.append(line)
    extra = jnp.concatenate(lines, axis=0).astype(BF16)
    values = (volt_ref[:, 0, :], volt_ref[:, 1, :])
    depth = out_ref.shape[0] // peers
    for peer in range(peers):
        line = peer * depth
        for value in values:
            for start in range(side_of(peer) * part, (side_of(peer) + 1) * part, LANES):
                out_ref[line : line + stations, :] = value[:, start : start + LANES]
                line += stations
        out_ref[line : line + 2, :] = extra


def spread(first, high, low):
    offset = lax.broadcasted_iota(jnp.int32, (GRID, first.shape[1]), 0).astype(F32) - first
    offset = offset.astype(BF16)
    high, low = high.astype(BF16), low.astype(BF16)
    out_high = jnp.zeros_like(offset)
    out_low = jnp.zeros_like(offset)
    for k in range(high.shape[0]):
        hit = offset == jnp.asarray(k, BF16)
        out_high = jnp.where(hit, high[k : k + 1], out_high)
        out_low = jnp.where(hit, low[k : k + 1], out_low)
    return out_high, out_low


def respond(table, high, low):
    return (
        jnp.dot(table[:, :GRID], high, preferred_element_type=F32)
        + jnp.dot(table[:, GRID:], high, preferred_element_type=F32)
        + jnp.dot(table[:, :GRID], low, preferred_element_type=F32)
    )


def image_kernel(taps, share, split, scale, row_of, gathered_ref, tail_ref, tables_ref, weight_ref, send_ref,
                 corr_ref, rows_ref, beam_a, beam_b, exact_a, exact_b, column_ref, volts_ref):
    sources = tail_ref.shape[0]
    local = LANES // (4 * taps)
    stations = sources * local
    lines = gathered_ref.shape[0] // sources
    tiles = (lines - 2) // local // 2
    for source in range(sources):
        for tile in range(2 * tiles):
            start = source * lines + tile * local
            volts_ref[source * local : (source + 1) * local, tile * LANES : (tile + 1) * LANES] = (
                gathered_ref[start : start + local, :]
            )
    samples = tiles * LANES
    depth = GRID // LANES * share + 1
    peers = send_ref.shape[0] // (depth * split)
    per_peer = weight_ref.shape[1] // peers
    columns = share * split
    row = row_of()

    both = volts_ref[...]
    real = volts_ref[:, :samples]
    imag = volts_ref[:, samples:]
    outer = (((1,), (1,)), ((), ()))
    corr_ref[stations:] = lax.dot_general(both, both, outer, preferred_element_type=F32).astype(BF16)
    turned = lax.dot_general(real, imag, outer, preferred_element_type=F32)
    turned -= lax.dot_general(imag, real, outer, preferred_element_type=F32)
    corr_ref[:stations] = (2.0 * turned).astype(BF16)

    source = lax.broadcasted_iota(jnp.int32, (sources, stations), 0)
    station = lax.broadcasted_iota(jnp.int32, (sources, stations), 1)
    expand = jnp.where(station // local == source, 1.0, 0.0).astype(BF16)
    place = lax.broadcasted_iota(jnp.int32, (LANES, stations), 0) % local
    wanted = place == lax.broadcasted_iota(jnp.int32, (LANES, stations), 1) % local
    extras = []
    for part in range(2):
        spots = lax.dot_general(
            tail_ref[:, tail_ref.shape[1] - 1, part, :], expand, (((0,), (0,)), ((), ())), preferred_element_type=F32
        )
        spots = jnp.where(wanted, spots, 0.0).reshape(LANES // local, local, stations)
        extras.append(jnp.sum(spots, axis=1))
    high, low, first = extras[0][: 2 * taps], extras[0][2 * taps :], extras[1][:2]
    row_high, row_low = spread(first[:1], high[:taps], low[:taps])
    col_high, col_low = spread(first[1:], high[taps:], low[taps:])
    rows_ref[...] = respond(tables_ref[...], row_high, row_low)
    run = share * SPLIT_Z
    bases = [pl.multiple_of(first * share, run) for first in neighbours(row)[::SPLIT_Z]]
    mine = [tables_ref[pl.ds(part + base, run), :] for part in (0, GRID) for base in bases]
    column = respond(jnp.concatenate(mine, axis=0), col_high, col_low)
    column_cos, column_sin = column[:columns], column[columns:]

    slots = ((beam_a, exact_a), (beam_b, exact_b))

    group = beam_a.shape[0] // GRID

    def build(step):
        beam, exact = slots[step % 2]
        r_real, r_imag = rows_ref[:GRID], rows_ref[GRID:]
        for j in range(group):
            m = step * group + j
            lines = slice(j * GRID, (j + 1) * GRID)
            c_real, c_imag = column_cos[m : m + 1], column_sin[m : m + 1]
            beam_real = c_real * r_real - c_imag * r_imag
            beam_imag = c_real * r_imag + c_imag * r_real
            exact[0, lines] = beam_real
            exact[1, lines] = beam_imag
            beam[lines, :stations] = beam_real.astype(BF16)
            beam[lines, stations:] = beam_imag.astype(BF16)

    build(0)
    steps = columns // group
    for step in range(steps):
        beam, exact = slots[step % 2]
        sum_real = jnp.dot(beam[:, :stations], corr_ref[stations:], preferred_element_type=F32)
        product = exact[0] * sum_real
        total = product[:, :LANES] + product[:, LANES:]
        sum_imag = jnp.dot(beam[...], corr_ref[...], preferred_element_type=F32)
        if step + 1 < steps:
            build(step + 1)
        product = exact[1] * sum_imag
        total += product[:, :LANES] + product[:, LANES:]
        power = jnp.sum(total, axis=1, keepdims=True) * scale
        for j in range(group):
            m = step * group + j
            column_ref[:, m : m + 1] = power[j * GRID : (j + 1) * GRID]
    power = column_ref[...].T
    weights = weight_ref[...]
    for peer in range(peers):
        own = weights[:, peer * per_peer : (peer + 1) * per_peer]
        own = jnp.concatenate([own, jnp.zeros((1, LANES - per_peer), F32)], axis=1)
        for side in range(split):
            start = (peer * split + side) * depth
            for half in range(GRID // LANES):
                lines = power[side * share : (side + 1) * share, half * LANES : (half + 1) * LANES]
                send_ref[start + half * share : start + (half + 1) * share, :] = lines
            send_ref[start + depth - 1 : start + depth, :] = own


def finish_kernel(split, channel_of, parts_ref, power_ref, maps_ref):
    share = power_ref.shape[0]
    per_peer = maps_ref.shape[0] // share
    halves = GRID // LANES
    depth = halves * share + 1
    channel = channel_of()
    blocks = parts_ref.shape[0] // depth
    power = jnp.zeros((halves * share, LANES), F32)
    maps = [power] * per_peer
    for block in range(blocks):
        start = block * depth
        part = parts_ref[start : start + depth - 1, :]
        weights = parts_ref[start + depth - 1 : start + depth, :]
        power += jnp.where(channel == block // split, part, 0.0)
        for q in range(per_peer):
            maps[q] += part * weights[:, q : q + 1]
    for half in range(halves):
        lanes = slice(half * LANES, (half + 1) * LANES)
        lines = slice(half * share, (half + 1) * share)
        power_ref[:, lanes] = power[lines]
        for q in range(per_peer):
            maps_ref[q * share : (q + 1) * share, lanes] = maps[q][lines]


def vmem():
    return pl.BlockSpec(memory_space=pltpu.VMEM)


def packed(volt, kern, foot, gain, peers, split):
    stations, _, samples = volt.shape
    inputs = [pltpu.with_memory_space_constraint(x, pltpu.HBM) for x in (volt, kern, foot, gain)]
    return pl.pallas_call(
        functools.partial(pack_kernel, peers, split),
        out_shape=(
            jax.ShapeDtypeStruct((peers * (stations * 2 * samples // split // LANES + 2), LANES), BF16),
            jax.ShapeDtypeStruct(gain.shape, F32),
        ),
        in_specs=[pl.BlockSpec(memory_space=pltpu.HBM)] * 4,
        out_specs=(vmem(), vmem()),
        scratch_shapes=[
            pltpu.VMEM((LANES, LANES), F32),
            pltpu.VMEM(volt.shape, volt.dtype),
            pltpu.VMEM(kern.shape, kern.dtype),
            pltpu.VMEM(foot.shape, foot.dtype),
            pltpu.SemaphoreType.DMA((4,)),
        ],
        compiler_params=pltpu.CompilerParams(vmem_limit_bytes=8 << 20),
        name="pack",
    )(*inputs)


def imaged(gathered, tail, tables, weight, peers, taps, share, split, scale, row_of, interpret=False):
    sources = tail.shape[0]
    stations = sources * (LANES // (4 * taps))
    width = (gathered.shape[0] // sources - 2) * LANES // (stations // sources)
    return pl.pallas_call(
        functools.partial(image_kernel, taps, share, split, scale, row_of),
        out_shape=jax.ShapeDtypeStruct((peers * split * (share * GRID // LANES + 1), LANES), F32),
        in_specs=[vmem()] * 4,
        out_specs=vmem(),
        scratch_shapes=[
            pltpu.VMEM((2 * stations, stations), BF16),
            pltpu.VMEM((2 * GRID, stations), F32),
            pltpu.VMEM((GROUP * GRID, 2 * stations), BF16),
            pltpu.VMEM((GROUP * GRID, 2 * stations), BF16),
            pltpu.VMEM((2, GROUP * GRID, stations), F32),
            pltpu.VMEM((2, GROUP * GRID, stations), F32),
            pltpu.VMEM((GRID, LANES), F32),
            pltpu.VMEM((stations, width), BF16),
        ],
        compiler_params=pltpu.CompilerParams(vmem_limit_bytes=32 << 20),
        name="image",
        interpret=interpret,
    )(gathered, tail, tables, weight)


def finished(parts, share, per_peer, split, channel_of, interpret=False):
    return pl.pallas_call(
        functools.partial(finish_kernel, split, channel_of),
        out_shape=(
            jax.ShapeDtypeStruct((share, GRID), F32),
            jax.ShapeDtypeStruct((per_peer * share, GRID), F32),
        ),
        in_specs=[vmem()],
        out_specs=(vmem(), vmem()),
        compiler_params=pltpu.CompilerParams(vmem_limit_bytes=8 << 20),
        name="finish",
        interpret=interpret,
    )(parts)


def on_device(tables, voltages, kernels, footprint, cal_weight):
    local_stations, _, local_channels, samples = voltages.shape
    rows = lax.axis_size("row")
    channels = lax.axis_size("chan")
    share = GRID // rows
    taps = kernels.shape[2]
    station_count = local_stations * rows
    scale = 1.0 / (2.0 * samples * station_count * taps * taps)
    volt = voltages.reshape(local_stations, 2, samples)
    kern = jnp.transpose(kernels, (1, 2, 0))
    send, weight = packed(volt, kern, footprint.T, cal_weight.T, rows, SPLIT)
    send = send.reshape(rows, -1, 2, LANES)
    blocks = lax.all_to_all(send, "row", 0, 0, tiled=True)
    gathered = blocks.reshape(-1, LANES)
    weighted = imaged(
        gathered, blocks, tables, weight, channels, taps, share, SPLIT, scale,
        lambda: lax.axis_index("row"),
    )
    groups = [
        [c * rows + near for c in range(channels) for near in neighbours(row)]
        for row in range(rows)
        if side_of(row) == 0
    ]
    weighted = weighted.reshape(channels * SPLIT, 1, -1)
    parts = lax.all_to_all(
        weighted, ("chan", "row"), 0, 0, axis_index_groups=groups, tiled=True
    )
    parts = parts.reshape(-1, LANES)
    power, maps = finished(parts, share, weight.shape[1] // channels, SPLIT, lambda: lax.axis_index("chan"))
    maps = maps.reshape(-1, share, GRID)
    return jnp.transpose(power[None], (0, 2, 1)), jnp.transpose(maps, (0, 2, 1))


def solution(mesh):
    specs = (P("row", None, "chan", None), P("row", None, None), P("row", None), P(None, "chan"))
    tables = transform_tables()
    return jax.shard_map(
        lambda *args: on_device(jnp.asarray(tables), *args),
        mesh=mesh,
        in_specs=specs,
        out_specs=(P("chan", None, "row"), P("chan", None, "row")),
        check_vma=False,
    )
```
